512 devices in a mesh: row: 64 (over y, z_hi, core), hid: 8 (over z_lo, x).
Axes of the slice: x: 4, y: 8, z: 8 (z_hi: 4, z_lo: 2; z = z_hi * 2 + z_lo), core: 2. Of those that a mesh axis runs over, the one named last changes fastest.
Arguments:
- features: bfloat16 [256, 256, 512], P('row'), may hold values from -6 to 6
- dw_weight: float32 [2, 7, 7, 512], replicated, may hold values from -0.875 to 0.875
- dw_bias: float32 [2, 512], replicated, may hold values from -3 to 3
- ln_gain: float32 [2, 512], replicated, may hold values from 0.1 to 1.9
- ln_bias: float32 [2, 512], replicated, may hold values from -3 to 3
- w_up: bfloat16 [2, 512, 2048], P(None, None, 'hid'), may hold values from -0.25 to 0.25
- b_up: float32 [2, 2048], P(None, 'hid'), may hold values from -3 to 3
- w_down: bfloat16 [2, 2048, 512], P(None, 'hid'), may hold values from -0.125 to 0.125
- b_down: float32 [2, 512], replicated, may hold values from -3 to 3
- layer_scale: float32 [2, 512], replicated, may hold values from 0.2 to 1
Outputs:
- result_map: bfloat16 [256, 256, 512], P('row')
The draws below stay inside these ranges and needn't reach their ends.
All inputs are finite; a program needn't handle non-finite values.
Results may differ from the reference program's by a relative error of at most 0.018.
Values may be sent and summed in bfloat16 or wider, within the bound.
A program may use at most 64 MiB of HBM per device.

```python
import math
import jax
import jax.numpy as jnp
from jax import lax

C = 512
FF = 2048
WIDTH = 256
BLOCKS = 2
KSIZE = 7
HEIGHT = 256
FF_DEV = 256


def block_scale(stream_key, dims, shards, smallest, largest):
    loudness, own = 1.0, jax.random.fold_in(stream_key, 6)
    for position, parts in shards:
        heights = jnp.exp(jax.random.uniform(jax.random.fold_in(own, position), (parts,), jnp.float32, smallest / len(shards), largest / len(shards)))
        loudness = loudness * jnp.repeat(heights, dims[position] // parts).reshape([-1 if axis == position else 1 for axis in range(len(dims))])
    return loudness


def bell_draw(key, shape, scale, limit, shards=(), kind=jnp.bfloat16):
    drawn = jax.random.normal(key, shape, jnp.float32) * scale
    if len(shards) > 0:
        drawn = block_scale(key, shape, shards, -0.22, 0.18) * drawn
    return jnp.clip(drawn, min=-limit, max=limit).astype(kind)


def setup_inputs(seed: int = 0) -> dict:
    arg_keys = jax.random.split(jax.random.key(seed), 11)
    features = bell_draw(arg_keys[0], (HEIGHT, WIDTH, C), 1.0, 6.0, ((0, 64),))
    dw_weight = bell_draw(arg_keys[1], (BLOCKS, KSIZE, KSIZE, C), (KSIZE * KSIZE) ** -0.5, 0.875, (), jnp.float32)
    dw_bias = bell_draw(arg_keys[2], (BLOCKS, C), 0.5, 3.0, (), jnp.float32)
    ln_gain = jnp.clip(1.0 + 0.18 * jax.random.normal(arg_keys[3], (BLOCKS, C), jnp.float32), 0.1, 1.9)
    ln_bias = bell_draw(arg_keys[4], (BLOCKS, C), 0.5, 3.0, (), jnp.float32)
    w_up = bell_draw(arg_keys[5], (BLOCKS, C, FF), C ** -0.5, 0.25, ((2, 8),))
    b_up = bell_draw(arg_keys[6], (BLOCKS, FF), 0.5, 3.0, ((1, 8),), jnp.float32)
    w_down = bell_draw(arg_keys[7], (BLOCKS, FF, C), FF ** -0.5, 0.125, ((1, 8),))
    b_down = bell_draw(arg_keys[8], (BLOCKS, C), 0.5, 3.0, (), jnp.float32)
    layer_scale = jnp.clip(jnp.exp(jax.random.uniform(arg_keys[9], (BLOCKS, C), jnp.float32, math.log(0.2), math.log(1.0))), 0.2, 1.0)
    return {"features": features, "dw_weight": dw_weight, "dw_bias": dw_bias, "ln_gain": ln_gain, "ln_bias": ln_bias, "w_up": w_up, "b_up": b_up, "w_down": w_down, "b_down": b_down, "layer_scale": layer_scale}


def depthwise(state, kernel, bias):
    pad = KSIZE // 2
    padded = jnp.pad(state.astype(jnp.float32), ((pad, pad), (pad, pad), (0, 0)))
    height, width = (state.shape[0], state.shape[1])
    total = jnp.zeros(state.shape, jnp.float32)
    for i in range(KSIZE):
        for j in range(KSIZE):
            total = total + padded[i:i + height, j:j + width, :] * kernel[i, j]
    return (total + bias).astype(jnp.bfloat16)

def reference(features, dw_weight, dw_bias, ln_gain, ln_bias, w_up, b_up, w_down, b_down, layer_scale):
    state = features
    for b in range(BLOCKS):
        conv = depthwise(state, dw_weight[b], dw_bias[b]).reshape(-1, C)
        values = conv.astype(jnp.float32)
        mean = lax.optimization_barrier(jnp.mean(values, axis=1, keepdims=True))
        var = lax.optimization_barrier(jnp.mean((values - mean) ** 2, axis=1, keepdims=True))
        normed = ((values - mean) / jnp.sqrt(var + 1e-06) * ln_gain[b] + ln_bias[b]).astype(jnp.bfloat16)
        hidden = jax.nn.gelu(jnp.dot(normed, w_up[b], preferred_element_type=jnp.float32) + b_up[b], approximate=False).astype(jnp.bfloat16)
        projected = jnp.zeros((hidden.shape[0], C), jnp.float32)
        for g in range(FF // FF_DEV):
            part = jnp.dot(hidden[:, g * FF_DEV:(g + 1) * FF_DEV], w_down[b, g * FF_DEV:(g + 1) * FF_DEV, :], preferred_element_type=jnp.float32)
            projected = projected + part.astype(jnp.bfloat16).astype(jnp.float32)
        flat = state.reshape(-1, C).astype(jnp.float32)
        state = (flat + layer_scale[b] * (projected + b_down[b])).astype(jnp.bfloat16).reshape(state.shape)
    return state
```

```python
import functools

import jax
import jax.numpy as jnp
from jax import lax
from jax.experimental import pallas as pl
from jax.experimental.pallas import tpu as pltpu
from jax.sharding import PartitionSpec as P

MESH = pl.DeviceIdType.MESH
C, F, COLS, OWN, WIDE = 512, 256, 256, 32, 48
X, Y, ZH = 4, 8, 4
LANES = C // 128


def kernel(
    features, dww, dwb, gain, shift, w_up, b_up, w_down, b_down, scale, out,
    w, bup, xin, xf, conv, normed, acc, state, halo,
    load_sem, x1_send, x1_recv, x2_send, x2_recv, z_send, z_recv, y_send, y_recv, p_send, p_recv,
    b_send, b_recv, f_send, f_recv, h_send, h_recv, g_send, g_recv,
):
    row, hid = lax.axis_index("row"), lax.axis_index("hid")
    y, zh, core = row // 8, (row // 2) % 4, row % 2
    zl, x = hid // 4, hid % 4
    parity = y % 2

    def at(r, h):
        return {"row": r, "hid": h}

    def share(k):
        kk = k % 4
        return ((zl + k // 4) % 2) * 4 + (x + kk + (kk // 2) * (5 - 2 * kk)) % 4

    def place(h):
        return (h // 4) * 7 + (1 - 2 * (h // 4)) * (h % 4)

    right, left = at(row, zl * 4 + (x + 1) % 4), at(row, zl * 4 + (x + 3) % 4)
    twin = at(row, (1 - zl) * 4 + x)
    zh_up, zh_down = (zh + zl) % 4, (zh + 3 + zl) % 4
    z_up = at(y * 8 + zh_up * 2 + core, (1 - zl) * 4 + x)
    z_down = at(y * 8 + zh_down * 2 + core, (1 - zl) * 4 + x)
    y_up, y_down = at((row + 8) % 64, hid), at((row + 56) % 64, hid)
    partner = at(y * 8 + zh * 2 + 1 - core, hid)
    below, above = at((row + 1) % 64, hid), at((row + 63) % 64, hid)
    peers = [at(row, (hid + d) % 8) for d in range(1, 8)]
    far_z = at(y * 8 + ((zh + 3 + 2 * zl) % 4) * 2 + core, (1 - zl) * 4 + x)
    far_row = at((row + 63 + 2 * core) % 64, hid)

    mine = place(hid)
    start = jnp.clip(mine * OWN - 16, 0, COLS - 64)
    into = pl.multiple_of(start - mine * OWN + 32, 16)
    start = pl.multiple_of(start, 16)

    loads = []
    for b in range(2):
        for c in range(2):
            loads.append((w_up.at[b, pl.ds(256 * c, 256), :], w.at[b, hid, c, 0:256, :], load_sem.at[4 * b + 2 * c]))
            loads.append((w_down.at[b, :, pl.ds(256 * c, 256)], w.at[b, hid, c, 256:512, :], load_sem.at[4 * b + 2 * c + 1]))
    loads.append((features.at[:, pl.ds(start, 64), :], xin.at[3:7, pl.ds(into, 64), :], load_sem.at[8]))
    loads.append((b_up, bup.at[hid], load_sem.at[9]))
    loads = [pltpu.make_async_copy(*load) for load in loads]
    for load in loads:
        load.start()

    @pl.when(mine == 0)
    def _():
        xin[:, 16:32, :] = jnp.zeros((10, 16, C), jnp.bfloat16)

    @pl.when(mine == 7)
    def _():
        xin[:, 64:80, :] = jnp.zeros((10, 16, C), jnp.bfloat16)

    barrier = pltpu.get_barrier_semaphore()
    greeted = peers + [far_z, y_up, y_down, partner, far_row]
    for device in greeted:
        pl.semaphore_signal(barrier, inc=1, device_id=device, device_id_type=MESH)
    pl.semaphore_wait(barrier, len(greeted))

    sent = []

    def send(src, dst, send_sem, recv_sem, device):
        copy = pltpu.make_async_remote_copy(
            src_ref=src, dst_ref=dst, send_sem=send_sem, recv_sem=recv_sem, device_id=device, device_id_type=MESH
        )
        copy.start()
        sent.append(copy)

    def arrived(dst, send_sem, recv_sem):
        pltpu.make_async_remote_copy(
            src_ref=dst, dst_ref=dst, send_sem=send_sem, recv_sem=recv_sem, device_id=partner, device_id_type=MESH
        ).wait_recv()

    def part(b, k, at_core, first=0, count=512):
        return w.at[b, share(k), at_core, pl.ds(first, count), :]

    def pass_on(ref, send_sem, recv_sem, device):
        send(ref, ref, send_sem, recv_sem, device)

    def x1(b):
        pass_on(part(b, 0, core, 0, 256), x1_send.at[b, 0], x1_recv.at[b, 0], right)
        pass_on(part(b, 0, core, 256, 256), x1_send.at[b, 2], x1_recv.at[b, 2], left)
        pass_on(part(b, 0, core, 256, 256), x1_send.at[b, 1], x1_recv.at[b, 1], right)
        pass_on(part(b, 0, core, 0, 256), x1_send.at[b, 3], x1_recv.at[b, 3], left)

    def x2(b):
        arrived(part(b, 2, core, 0, 256), x1_send.at[b, 0], x1_recv.at[b, 0])
        pass_on(part(b, 2, core, 0, 256), x2_send.at[b, 0], x2_recv.at[b, 0], right)
        arrived(part(b, 1, core, 256, 256), x1_send.at[b, 2], x1_recv.at[b, 2])
        pass_on(part(b, 1, core, 256, 256), x2_send.at[b, 1], x2_recv.at[b, 1], left)

    def x1_rest(b):
        arrived(part(b, 2, core, 256, 256), x1_send.at[b, 1], x1_recv.at[b, 1])
        arrived(part(b, 1, core, 0, 256), x1_send.at[b, 3], x1_recv.at[b, 3])

    def x2_rest(b):
        arrived(part(b, 3, core, 0, 256), x2_send.at[b, 0], x2_recv.at[b, 0])
        arrived(part(b, 3, core, 256, 256), x2_send.at[b, 1], x2_recv.at[b, 1])

    def quarter(b, k, near, from_up):
        first = 256 * (parity if near else 1 - parity) + 128 * from_up
        return part(b, k, core, pl.multiple_of(first, 128), 128)

    def z(b, k):
        pass_on(quarter(b, k, True, 0), z_send.at[b, k, 0], z_recv.at[b, k, 0], z_up)
        pass_on(quarter(b, k, True, 1), z_send.at[b, k, 1], z_recv.at[b, k, 1], z_down)

    def yy(b, k):
        arrived(quarter(b, k + 4, True, 0), z_send.at[b, k, 0], z_recv.at[b, k, 0])
        pass_on(quarter(b, k + 4, True, 0), y_send.at[b, k, 0], y_recv.at[b, k, 0], y_up)
        arrived(quarter(b, k + 4, True, 1), z_send.at[b, k, 1], z_recv.at[b, k, 1])
        pass_on(quarter(b, k + 4, True, 1), y_send.at[b, k, 1], y_recv.at[b, k, 1], y_down)

    def y_rest(b, k):
        for side in range(2):
            arrived(quarter(b, k + 4, False, side), y_send.at[b, k, side], y_recv.at[b, k, side])

    def to_partner(b, k):
        pass_on(part(b, k, core), p_send.at[b, k - 1], p_recv.at[b, k - 1], partner)

    def from_partner(b, k):
        arrived(part(b, k, 1 - core), p_send.at[b, k - 1], p_recv.at[b, k - 1])

    for load in loads:
        load.wait()
    x1(0)
    z(0, 0)
    window = xin.at[3:7, pl.ds(into, 64), :]
    send(xin.at[4:7, pl.ds(into, 64), :], xin.at[0:3, pl.ds(into, 64), :], f_send.at[0], f_recv.at[0], below)
    send(xin.at[3:6, pl.ds(into, 64), :], xin.at[7:10, pl.ds(into, 64), :], f_send.at[1], f_recv.at[1], above)
    for n, peer in enumerate(peers):
        send(bup.at[hid], bup.at[hid], b_send.at[n], b_recv.at[n], peer)

    def convolve(b, columns, offset):
        def one(g, _):
            lanes = pl.ds(pl.multiple_of(g * 128, 128), 128)
            total = [jnp.zeros((columns, 128), jnp.float32) + dwb[b : b + 1, lanes] for _ in range(4)]
            for j in range(7):
                for i in range(10):
                    value = xf[g, i, pl.ds(offset - 3 + j, columns), :]
                    for r in range(max(0, i - 6), min(3, i) + 1):
                        total[r] = total[r] + value * dww[b, i - r, j : j + 1, lanes]
            for r in range(4):
                conv[pl.ds(r * columns, columns), lanes] = total[r]
            return 0

        lax.fori_loop(0, LANES, one, 0)

        def norm(t, _):
            rows = pl.ds(pl.multiple_of(t * 32, 32), 32)
            values = conv[rows, :].astype(jnp.bfloat16).astype(jnp.float32)
            mean = jnp.mean(values, axis=1, keepdims=True)
            var = jnp.mean((values - mean) ** 2, axis=1, keepdims=True)
            result = (values - mean) / jnp.sqrt(var + 1e-06) * gain[b : b + 1, :] + shift[b : b + 1, :]
            normed[rows, :] = result.astype(jnp.bfloat16)
            return 0

        lax.fori_loop(0, columns * 4 // 32, norm, 0)
        acc[0 : columns * 4, :] = jnp.zeros((columns * 4, C), jnp.float32) + b_down[b : b + 1, :]

    def pointwise(b, count, first, last):
        def one(k, _):
            s = share(k)
            up = jnp.dot(normed[0:count, 0:256], w[b, s, 0, 0:256, :], preferred_element_type=jnp.float32)
            up = up + jnp.dot(normed[0:count, 256:512], w[b, s, 1, 0:256, :], preferred_element_type=jnp.float32)
            up = up + bup[s, b : b + 1, :]
            hidden = (0.5 * up * (1.0 + lax.erf(up * 0.5**0.5))).astype(jnp.bfloat16)
            for c in range(2):
                lanes = slice(256 * c, 256 * c + 256)
                acc[0:count, lanes] += jnp.dot(hidden, w[b, s, c, 256:512, :], preferred_element_type=jnp.float32)
            return 0

        lax.fori_loop(first, last, one, 0)

    for side in range(2):
        arrived(xin.at[pl.ds(7 * side, 3), pl.ds(into, 64), :], f_send.at[side], f_recv.at[side])

    @pl.when(row == 0)
    def _():
        xin[0:3, :, :] = jnp.zeros((3, 96, C), jnp.bfloat16)

    @pl.when(row == 63)
    def _():
        xin[7:10, :, :] = jnp.zeros((3, 96, C), jnp.bfloat16)

    def widen(i, _):
        for g in range(LANES):
            xf[g, i, :, :] = xin[i, 16:80, 128 * g : 128 * g + 128].astype(jnp.float32)
        return 0

    lax.fori_loop(0, 10, widen, 0)
    convolve(0, WIDE, 8)
    x2(0)
    x1(1)
    z(1, 0)
    yy(0, 0)
    for n, peer in enumerate(peers):
        origin = (hid + 7 - n) % 8
        arrived(bup.at[origin], b_send.at[n], b_recv.at[n])
    pointwise(0, 4 * WIDE, 0, 1)
    x1_rest(0)
    for k in (1, 2):
        z(0, k)
        to_partner(0, k)
    y_rest(0, 0)
    to_partner(0, 4)
    x2_rest(0)
    z(0, 3)
    to_partner(0, 3)
    yy(0, 1)
    yy(0, 2)
    yy(1, 0)
    for k in (1, 2):
        from_partner(0, k)
    pointwise(0, 4 * WIDE, 1, 3)
    x2(1)
    yy(0, 3)
    for k in (1, 2):
        y_rest(0, k)
        to_partner(0, k + 4)
    from_partner(0, 3)
    from_partner(0, 4)
    pointwise(0, 4 * WIDE, 3, 5)
    y_rest(0, 3)
    to_partner(0, 7)
    y_rest(1, 0)
    to_partner(1, 4)
    for k in (5, 6, 7):
        from_partner(0, k)
    pointwise(0, 4 * WIDE, 5, 8)

    def settle(r, _):
        rows = pl.ds(pl.multiple_of(r * WIDE, WIDE), WIDE)
        old = xin[3 + r, 24:72, :].astype(jnp.float32)
        new = (old + scale[0:1, :] * acc[rows, :]).astype(jnp.bfloat16)
        column = mine * OWN - 8 + lax.broadcasted_iota(jnp.int32, (WIDE, C), 0)
        new = jnp.where((column >= 0) & (column < COLS), new, jnp.zeros_like(new))
        state[r, :, :] = new
        for g in range(LANES):
            xf[g, 3 + r, 0:WIDE, :] = new[:, 128 * g : 128 * g + 128].astype(jnp.float32)
        return 0

    lax.fori_loop(0, 4, settle, 0)
    send(state.at[1:4], halo.at[0], h_send.at[0], h_recv.at[0], below)
    send(state.at[0:3], halo.at[1], h_send.at[1], h_recv.at[1], above)
    x1_rest(1)
    for k in (1, 2):
        z(1, k)
        to_partner(1, k)
    for side in range(2):
        arrived(halo.at[side], h_send.at[side], h_recv.at[side])

    @pl.when(row == 0)
    def _():
        halo[0, :, :, :] = jnp.zeros((3, WIDE, C), jnp.bfloat16)

    @pl.when(row == 63)
    def _():
        halo[1, :, :, :] = jnp.zeros((3, WIDE, C), jnp.bfloat16)

    def widen_halo(i, _):
        for side in range(2):
            for g in range(LANES):
                xf[g, 7 * side + i, 0:WIDE, :] = halo[side, i, :, 128 * g : 128 * g + 128].astype(jnp.float32)
        return 0

    lax.fori_loop(0, 3, widen_halo, 0)
    yy(1, 1)
    yy(1, 2)
    convolve(1, OWN, 8)
    pointwise(1, 4 * OWN, 0, 1)
    x2_rest(1)
    z(1, 3)
    to_partner(1, 3)
    for k in (1, 2):
        y_rest(1, k)
        to_partner(1, k + 4)
    from_partner(1, 1)
    from_partner(1, 2)
    pointwise(1, 4 * OWN, 1, 3)
    yy(1, 3)
    from_partner(1, 3)
    from_partner(1, 4)
    pointwise(1, 4 * OWN, 3, 5)
    y_rest(1, 3)
    to_partner(1, 7)
    from_partner(1, 5)
    from_partner(1, 6)
    pointwise(1, 4 * OWN, 5, 7)
    from_partner(1, 7)
    pointwise(1, 4 * OWN, 7, 8)

    def columns_of(h, rows=slice(0, 4)):
        return out.at[rows, pl.ds(pl.multiple_of(place(h) * OWN, OWN), OWN), :]

    def finish(r, _):
        rows = pl.ds(pl.multiple_of(r * OWN, OWN), OWN)
        old = state[r, 8:40, :].astype(jnp.float32)
        new = (old + scale[1:2, :] * acc[rows, :]).astype(jnp.bfloat16)
        out[r, pl.ds(pl.multiple_of(mine * OWN, OWN), OWN), :] = new
        return 0

    lax.fori_loop(0, 4, finish, 0)
    first, second = slice(0, 2), slice(2, 4)

    def get(k, rows, n):
        arrived(columns_of(share(k), rows), g_send.at[n], g_recv.at[n])

    def give(k, rows, n, device):
        pass_on(columns_of(share(k), rows), g_send.at[n], g_recv.at[n], device)

    give(0, slice(0, 4), 0, twin)
    give(0, first, 1, right)
    give(0, second, 3, left)
    give(0, second, 2, right)
    give(0, first, 4, left)
    get(2, first, 1)
    give(2, first, 5, right)
    get(1, second, 3)
    give(1, second, 6, left)
    get(4, slice(0, 4), 0)
    give(4, slice(0, 4), 7, right)
    give(4, slice(0, 4), 8, left)
    get(3, first, 5)
    give(3, first, 9, twin)
    get(3, second, 6)
    give(3, second, 10, twin)
    get(2, second, 2)
    get(1, first, 4)
    get(6, slice(0, 4), 7)
    get(5, slice(0, 4), 8)
    get(7, first, 9)
    get(7, second, 10)
    for copy in sent:
        copy.wait_send()


def tile(features, dw_weight, dw_bias, ln_gain, ln_bias, w_up, b_up, w_down, b_down, layer_scale):
    vmem, anywhere = pl.BlockSpec(memory_space=pltpu.VMEM), pl.BlockSpec(memory_space=pl.ANY)
    dma = pltpu.SemaphoreType.DMA
    pairs = [(2, 4), (2, 2), (2, 4, 2), (2, 4, 2), (2, 7), (7,), (2,), (2,), (11,)]
    return pl.pallas_call(
        kernel,
        out_shape=jax.ShapeDtypeStruct(features.shape, features.dtype),
        in_specs=[anywhere, vmem, vmem, vmem, vmem, anywhere, anywhere, anywhere, vmem, vmem],
        out_specs=vmem,
        scratch_shapes=[
            pltpu.VMEM((2, 8, 2, 512, 256), jnp.bfloat16),
            pltpu.VMEM((8, 2, F), jnp.float32),
            pltpu.VMEM((10, 96, C), jnp.bfloat16),
            pltpu.VMEM((LANES, 10, 64, 128), jnp.float32),
            pltpu.VMEM((4 * WIDE, C), jnp.float32),
            pltpu.VMEM((4 * WIDE, C), jnp.bfloat16),
            pltpu.VMEM((4 * WIDE, C), jnp.float32),
            pltpu.VMEM((4, WIDE, C), jnp.bfloat16),
            pltpu.VMEM((2, 3, WIDE, C), jnp.bfloat16),
            dma((10,)),
            *[dma(shape) for shape in pairs for _ in range(2)],
        ],
        compiler_params=pltpu.CompilerParams(collective_id=0, has_side_effects=True, vmem_limit_bytes=40 << 20),
    )(features, dw_weight, dw_bias, ln_gain, ln_bias, w_up, b_up, w_down, b_down, layer_scale)


def solution(mesh):
    return jax.shard_map(
        tile,
        mesh=mesh,
        in_specs=(
            P("row", None, None),
            P(),
            P(),
            P(),
            P(),
            P(None, None, "hid"),
            P(None, "hid"),
            P(None, "hid", None),
            P(),
            P(),
        ),
        out_specs=P("row", None, None),
        check_vma=False,
    )
```
